32 devices in a mesh: vec: 4 (over x, core), lat: 8 (over z, y).
Axes of the slice: x: 2, y: 2, z: 4, core: 2. Of those that a mesh axis runs over, the one named last changes fastest.
Arguments:
- perturbation: float32 [32, 3, 64, 2048], P('vec', None, 'lat'), may hold values from -6 to 6
- wind_coriolis: float32 [4, 3, 64, 2048], P(None, None, 'lat', 'vec'), may hold values from -4 to 4
- depth_field: float32 [4, 64, 2048], P(None, 'lat', 'vec'), may hold values from 0.5 to 2
Outputs:
- evolved: float32 [32, 3, 64, 2048], P('vec', None, 'lat')
The draws below stay inside these ranges and needn't reach their ends.
All inputs are finite; a program needn't handle non-finite values.
Results may differ from the reference program's by a relative error of at most 0.00002.
Values sent between devices are 32-bit elements; how exact they have to be, the bound alone decides.
A program may use at most 64 MiB of HBM per device.

```python
import math
import jax
import jax.numpy as jnp
from jax import lax

NLON = 2048
STEPS = 4
VECTORS = 32
NLAT = 64


def steps_of(rng, extent, split, smallest, top_value):
    def one(dim, blocks):
        steps = jax.random.uniform(jax.random.fold_in(jax.random.fold_in(rng, 6), dim), (blocks,), jnp.float32, smallest / len(split), top_value / len(split))
        return jnp.repeat(jnp.exp(steps), extent[dim] // blocks).reshape((-1,) + (1,) * (len(extent) - dim - 1))

    loudness = one(*split[0])
    for cut in split[1:]:
        loudness = loudness * one(*cut)
    return loudness


def scatter_about(key, extent, width, most, split=(), kind=jnp.bfloat16):
    values = jax.random.normal(key, extent, jnp.float32) * width
    if len(split) > 0:
        values = steps_of(key, extent, split, -0.22, 0.18) * values
    return jnp.clip(values, min=-most, max=most).astype(kind)


def setup_inputs(seed: int = 0) -> dict:
    streams_of = jax.random.split(jax.random.key(seed), 4)
    return {
        "perturbation": scatter_about(streams_of[0], (VECTORS, 3, NLAT, NLON), 1.0, 6.0, ((0, 4), (2, 8)), jnp.float32),
        "wind_coriolis": scatter_about(streams_of[1], (STEPS, 3, NLAT, NLON), 1.0, 4.0, ((2, 8), (3, 4)), jnp.float32),
        "depth_field": jnp.clip(jnp.exp(math.log(2.0) - 1.3862944 * jax.random.uniform(streams_of[2], (STEPS, NLAT, NLON), jnp.float32) ** steps_of(streams_of[2], (STEPS, NLAT, NLON), ((1, 8), (2, 4)), -0.2, 0.2)), 0.5, 2.0),
    }


time_step = 0.2
viscosity = 0.05


def lon_diff(field):
    return 0.5 * (jnp.roll(field, -1, axis=-1) - jnp.roll(field, 1, axis=-1))


def lat_diff(padded):
    return 0.5 * (padded[..., 2:, :] - padded[..., :-2, :])


def smooth(padded, centre):
    return padded[..., 2:, :] + padded[..., :-2, :] + jnp.roll(centre, -1, axis=-1) + jnp.roll(centre, 1, axis=-1) - 4.0 * centre


def advance(padded, coefficients):
    height_pad = padded[..., 0, :, :]
    zonal_pad = padded[..., 1, :, :]
    north_pad = padded[..., 2, :, :]
    height = height_pad[..., 1:-1, :]
    zonal = zonal_pad[..., 1:-1, :]
    north = north_pad[..., 1:-1, :]
    east_wind = coefficients[0]
    north_wind = coefficients[1]
    rotation = coefficients[2]
    depth_now = coefficients[3]
    tend_height = -(east_wind * lon_diff(height) + north_wind * lat_diff(height_pad) + depth_now * (lon_diff(zonal) + lat_diff(north_pad)))
    tend_zonal = -(east_wind * lon_diff(zonal) + north_wind * lat_diff(zonal_pad)) + rotation * north - lon_diff(height)
    tend_north = -(east_wind * lon_diff(north) + north_wind * lat_diff(north_pad)) - rotation * zonal - lat_diff(height_pad)
    new_height = height + time_step * (tend_height + viscosity * smooth(height_pad, height))
    new_zonal = zonal + time_step * (tend_zonal + viscosity * smooth(zonal_pad, zonal))
    new_north = north + time_step * (tend_north + viscosity * smooth(north_pad, north))
    return jnp.stack([new_height, new_zonal, new_north], axis=-3)


def reference(perturbation, wind_coriolis, depth_field):
    coefficients = jnp.concatenate([wind_coriolis, depth_field[:, None]], axis=1)

    def single(state):
        for moment in range(STEPS):
            padded = jnp.pad(state, ((0, 0), (1, 1), (0, 0)))
            state = advance(padded, coefficients[moment])
        return state

    return lax.map(single, perturbation)
```

```python
import functools

import jax
import jax.numpy as jnp
from jax import lax
from jax.experimental import pallas as pl
from jax.experimental.pallas import tpu as pltpu
from jax.sharding import PartitionSpec as P

MESH = pl.DeviceIdType.MESH
LANES = 128
time_step = 0.2
viscosity = 0.05
side_weight = time_step * viscosity
half_step = 0.5 * time_step


def sweep(load, store, coefficient, sides, tiles, keep):
    lane = lax.broadcasted_iota(jnp.int32, (8, LANES), 1)
    row = lax.broadcasted_iota(jnp.int32, (8, LANES), 0)
    first_lane, last_lane = lane == 0, lane == LANES - 1
    first_row, last_row = row == 0, row == 7
    known = {}

    def tile(side, field, t):
        key = (side, field, t)
        if key not in known:
            value = load(side, field, t % tiles)
            known[key] = (value, pltpu.roll(value, LANES - 1, 1), pltpu.roll(value, 1, 1))
        return known[key]

    for t in range(tiles):
        east, west, rise, fall, here = {}, {}, {}, {}, {}
        for field in range(3):
            turned = []
            for side in range(2):
                value = tile(side, field, t)[0] if side in sides else load(side, field, t)
                turned.append((pltpu.roll(value, 7, 0), pltpu.roll(value, 1, 0)))
            for side in sides:
                before, now, after = (tile(side, field, t + k) for k in (-1, 0, 1))
                here[side, field] = now[0]
                east[side, field] = jnp.where(last_lane, after[1], now[1])
                west[side, field] = jnp.where(first_lane, before[2], now[2])
                rise[side, field] = jnp.where(last_row, turned[1 - side][0], turned[side][0])
                fall[side, field] = jnp.where(first_row, turned[1 - side][1], turned[side][1])
        for side in sides:
            a = half_step * coefficient(side, 0, t)
            b = half_step * coefficient(side, 1, t)
            d = time_step * coefficient(side, 2, t)
            c = half_step * coefficient(side, 3, t)
            to_east, to_west = side_weight - a, side_weight + a
            to_rise, to_fall = side_weight - b, side_weight + b
            new = [
                (1.0 - 4.0 * side_weight) * here[side, f]
                + (to_east * east[side, f] + to_west * west[side, f])
                + (to_rise * rise[side, f] + to_fall * fall[side, f])
                for f in range(3)
            ]
            new[0] -= c * ((east[side, 1] - west[side, 1]) + (rise[side, 2] - fall[side, 2]))
            new[1] += d * here[side, 2] - half_step * (east[side, 0] - west[side, 0])
            new[2] -= d * here[side, 1] + half_step * (rise[side, 0] - fall[side, 0])
            for f in range(3):
                store(side, f, t, new[f] if side == 0 else jnp.where(keep, new[f], 0.0))


def kernel(
    nv, nl, x_hbm, wind, depth, out_hbm,
    x, halo, ping, pong, out, own, ring,
    x_sem, own_sem, out_sem,
    gs, gr, cs, cr, fs, fr, hs, hr,
):
    count, _, rows, width = x_hbm.shape
    steps, part = wind.shape[0], wind.shape[3]
    tiles, reach = width // LANES, steps
    v, l = lax.axis_index("vec"), lax.axis_index("lat")
    has = (l > 0, l < nl - 1)
    other = (l - 1, l + 1)
    peers = [lax.rem(v + k, nv) for k in range(1, nv)]
    edge = (lambda n: pl.ds(0, n), lambda n: pl.ds(rows - n, n))

    local = [
        pltpu.make_async_copy(x_hbm, x, x_sem.at[0]),
        pltpu.make_async_copy(wind, own.at[v, :, pl.ds(0, 3)], own_sem.at[0]),
        pltpu.make_async_copy(depth, own.at[v, :, 3], own_sem.at[1]),
    ]
    for copy in local:
        copy.start()

    for side in range(2):
        @pl.when(jnp.logical_not(has[1 - side]))
        def _(side=side):
            halo[:, :, edge[side](reach), :] = jnp.zeros((count, 3, reach, width), jnp.float32)

    barrier = pltpu.get_barrier_semaphore()
    for peer in peers:
        pl.semaphore_signal(barrier, inc=1, device_id={"vec": peer}, device_id_type=MESH)
    for side in range(2):
        @pl.when(has[side])
        def _(side=side):
            pl.semaphore_signal(barrier, inc=1, device_id={"lat": other[side]}, device_id_type=MESH)
    pl.semaphore_wait(barrier, nv - 1 + has[0].astype(jnp.int32) + has[1].astype(jnp.int32))

    def remote(src, dst, send, recv, target):
        return pltpu.make_async_remote_copy(
            src_ref=src, dst_ref=dst, send_sem=send, recv_sem=recv,
            device_id=target, device_id_type=MESH,
        )

    def edges(side):
        made = []
        for s in range(steps - 1):
            at = edge[side](reach - 1 - s)
            made.append(remote(
                wind.at[s, :, at, :], ring.at[v, s, pl.ds(0, 3), at, :],
                cs.at[side, s, 0], cr.at[side, s, 0], {"lat": other[side]}))
            made.append(remote(
                depth.at[s, at, :], ring.at[v, s, 3, at, :],
                cs.at[side, s, 1], cr.at[side, s, 1], {"lat": other[side]}))
        return made

    def state(side, k):
        at = edge[side](reach)
        return remote(
            x_hbm.at[k, :, at, :], halo.at[k, :, at, :],
            hs.at[side, k], hr.at[side, k], {"lat": other[side]})

    def spread(n, peer):
        return [
            remote(wind, own.at[v, :, pl.ds(0, 3)], gs.at[n, 0], gr.at[n, 0], {"vec": peer}),
            remote(depth, own.at[v, :, 3], gs.at[n, 1], gr.at[n, 1], {"vec": peer}),
        ]

    def passed(side, n, peer):
        made = []
        for s in range(steps - 1):
            at = edge[side](reach - 1 - s)
            made.append(remote(
                ring.at[v, s, :, at, :], ring.at[v, s, :, at, :],
                fs.at[side, n, s], fr.at[side, n, s], {"vec": peer}))
        return made

    for side in range(2):
        @pl.when(has[side])
        def _(side=side):
            for copy in edges(side):
                copy.start()

    @pl.loop(0, count)
    def _(k):
        for side in range(2):
            @pl.when(has[side])
            def _(side=side):
                state(side, k).start()

    for n, peer in enumerate(peers):
        for copy in spread(n, peer):
            copy.start()

    for side in range(2):
        @pl.when(has[1 - side])
        def _(side=side):
            for copy in edges(side):
                copy.wait_recv()
            for n, peer in enumerate(peers):
                for copy in passed(side, n, peer):
                    copy.start()

    for copy in local:
        copy.wait()
    for n, peer in enumerate(peers):
        for copy in spread(n, peer):
            copy.wait_recv()
    for side in range(2):
        @pl.when(has[1 - side])
        def _(side=side):
            for n, peer in enumerate(peers):
                for copy in passed(side, n, peer):
                    copy.wait_recv()

    row = lax.broadcasted_iota(jnp.int32, (8, LANES), 0)

    @pl.loop(0, count)
    def _(k):
        for side in range(2):
            @pl.when(has[1 - side])
            def _(side=side):
                state(side, k).wait_recv()

        def span(t):
            return pl.ds(t * LANES, LANES)

        def first(side, f, t):
            return (x, halo)[side][k, f, :, span(t)]

        def reader(ref):
            return lambda side, f, t: ref[side, f, :, span(t)]

        def writer(ref):
            def put(side, f, t, value):
                ref[side, f, :, span(t)] = value
            return put

        def last(side, f, t, value):
            out[k, f, :, span(t)] = value

        for s in range(steps):
            def coefficient(side, channel, t, s=s):
                block, offset = divmod(t * LANES, part)
                return (own, ring)[side][block, s, channel, :, pl.ds(offset, LANES)]

            final = s == steps - 1
            good = reach - 1 - s
            keep = ((row < good) & has[1]) | ((row >= rows - good) & has[0])
            sweep(
                first if s == 0 else reader((ping, pong)[(s - 1) % 2]),
                last if final else writer((ping, pong)[s % 2]),
                coefficient, (0,) if final else (0, 1), tiles, keep)
        pltpu.make_async_copy(out.at[k], out_hbm.at[k], out_sem.at[k]).start()

    for side in range(2):
        @pl.when(has[side])
        def _(side=side):
            for copy in edges(side):
                copy.wait_send()
        @pl.when(has[1 - side])
        def _(side=side):
            for n, peer in enumerate(peers):
                for copy in passed(side, n, peer):
                    copy.wait_send()
    for n, peer in enumerate(peers):
        for copy in spread(n, peer):
            copy.wait_send()

    @pl.loop(0, count)
    def _(k):
        for side in range(2):
            @pl.when(has[side])
            def _(side=side):
                state(side, k).wait_send()
        pltpu.make_async_copy(out.at[k], out_hbm.at[k], out_sem.at[k]).wait()


def solution(mesh):
    nv, nl = mesh.shape["vec"], mesh.shape["lat"]

    def shards(perturbation, wind_coriolis, depth_field):
        count, _, rows, width = perturbation.shape
        steps, part = wind_coriolis.shape[0], wind_coriolis.shape[3]
        dma = pltpu.SemaphoreType.DMA
        f32 = jnp.float32
        return pl.pallas_call(
            functools.partial(kernel, nv, nl),
            out_shape=jax.ShapeDtypeStruct(perturbation.shape, f32),
            in_specs=[pl.BlockSpec(memory_space=pl.ANY)] * 3,
            out_specs=pl.BlockSpec(memory_space=pl.ANY),
            scratch_shapes=[
                pltpu.VMEM((count, 3, rows, width), f32),
                pltpu.VMEM((count, 3, rows, width), f32),
                pltpu.VMEM((2, 3, rows, width), f32),
                pltpu.VMEM((2, 3, rows, width), f32),
                pltpu.VMEM((count, 3, rows, width), f32),
                pltpu.VMEM((nv, steps, 4, rows, part), f32),
                pltpu.VMEM((nv, steps - 1, 4, rows, part), f32),
                dma((1,)), dma((2,)), dma((count,)),
                dma((nv - 1, 2)), dma((nv - 1, 2)),
                dma((2, steps - 1, 2)), dma((2, steps - 1, 2)),
                dma((2, nv - 1, steps - 1)), dma((2, nv - 1, steps - 1)),
                dma((2, count)), dma((2, count)),
            ],
            compiler_params=pltpu.CompilerParams(
                collective_id=0, has_side_effects=True, vmem_limit_bytes=40 * 1024 * 1024
            ),
        )(perturbation, wind_coriolis, depth_field)

    placed = (P("vec", None, "lat", None), P(None, None, "lat", "vec"), P(None, "lat", "vec"))
    return jax.shard_map(
        shards, mesh=mesh, in_specs=placed, out_specs=P("vec", None, "lat", None), check_vma=False
    )
```

```python
import functools

import jax
import jax.numpy as jnp
from jax import lax
from jax.experimental import pallas as pl
from jax.experimental.pallas import tpu as pltpu
from jax.sharding import PartitionSpec as P

MESH = pl.DeviceIdType.MESH
LANES = 128
time_step = 0.2
viscosity = 0.05
side_weight = time_step * viscosity
half_step = 0.5 * time_step


def sweep(load, store, coefficient, sides, tiles, keep):
    lane = lax.broadcasted_iota(jnp.int32, (8, LANES), 1)
    row = lax.broadcasted_iota(jnp.int32, (8, LANES), 0)
    first_lane, last_lane = lane == 0, lane == LANES - 1
    first_row, last_row = row == 0, row == 7
    known = {}

    def tile(side, field, t):
        key = (side, field, t)
        if key not in known:
            value = load(side, field, t % tiles)
            known[key] = (value, pltpu.roll(value, LANES - 1, 1), pltpu.roll(value, 1, 1))
        return known[key]

    for t in range(tiles):
        east, west, rise, fall, here = {}, {}, {}, {}, {}
        for field in range(3):
            turned = []
            for side in range(2):
                value = tile(side, field, t)[0] if side in sides else load(side, field, t)
                turned.append((pltpu.roll(value, 7, 0), pltpu.roll(value, 1, 0)))
            for side in sides:
                before, now, after = (tile(side, field, t + k) for k in (-1, 0, 1))
                here[side, field] = now[0]
                east[side, field] = jnp.where(last_lane, after[1], now[1])
                west[side, field] = jnp.where(first_lane, before[2], now[2])
                rise[side, field] = jnp.where(last_row, turned[1 - side][0], turned[side][0])
                fall[side, field] = jnp.where(first_row, turned[1 - side][1], turned[side][1])
        for side in sides:
            a = half_step * coefficient(side, 0, t)
            b = half_step * coefficient(side, 1, t)
            d = time_step * coefficient(side, 2, t)
            c = half_step * coefficient(side, 3, t)
            to_east, to_west = side_weight - a, side_weight + a
            to_rise, to_fall = side_weight - b, side_weight + b
            new = [
                (1.0 - 4.0 * side_weight) * here[side, f]
                + (to_east * east[side, f] + to_west * west[side, f])
                + (to_rise * rise[side, f] + to_fall * fall[side, f])
                for f in range(3)
            ]
            new[0] -= c * ((east[side, 1] - west[side, 1]) + (rise[side, 2] - fall[side, 2]))
            new[1] += d * here[side, 2] - half_step * (east[side, 0] - west[side, 0])
            new[2] -= d * here[side, 1] + half_step * (rise[side, 0] - fall[side, 0])
            for f in range(3):
                store(side, f, t, new[f] if side == 0 else jnp.where(keep, new[f], 0.0))


def kernel(
    nv, nl, x_hbm, wind, depth, out_hbm,
    x, halo, transit, ping, pong, out, own, ring,
    x_sem, own_sem, out_sem,
    gs, gr, cs, cr, fs, fr, hs, hr, ts, tr,
):
    count, _, rows, width = x_hbm.shape
    steps, part = wind.shape[0], wind.shape[3]
    tiles, reach = width // LANES, steps
    v, l = lax.axis_index("vec"), lax.axis_index("lat")
    has = (l > 0, l < nl - 1)
    other = (l - 1, l + 1)
    far = (l - 2, l + 2)
    reaches = (l > 1, l < nl - 2)
    pairs = nl // 2
    odd = lax.rem(l, 2)
    place = l // 2

    def share(number, wanted):
        return jnp.where(wanted, number * count // pairs, 0) if nl % 2 == 0 else jnp.int32(0)

    relayed = (
        share(place, (odd == 0) & reaches[0]),
        share(pairs - 1 - place, (odd == 1) & reaches[1]),
    )
    relaying = (
        share(place, (odd == 1) & reaches[0]),
        share(pairs - 1 - place, (odd == 0) & reaches[1]),
    )
    peers = [lax.rem(v + k, nv) for k in range(1, nv)]
    edge = (lambda n: pl.ds(0, n), lambda n: pl.ds(rows - n, n))

    local = [
        pltpu.make_async_copy(x_hbm, x, x_sem.at[0]),
        pltpu.make_async_copy(wind, own.at[v, :, pl.ds(0, 3)], own_sem.at[0]),
        pltpu.make_async_copy(depth, own.at[v, :, 3], own_sem.at[1]),
    ]
    for copy in local:
        copy.start()

    for side in range(2):
        @pl.when(jnp.logical_not(has[1 - side]))
        def _(side=side):
            halo[:, :, edge[side](reach), :] = jnp.zeros((count, 3, reach, width), jnp.float32)

    barrier = pltpu.get_barrier_semaphore()
    for peer in peers:
        pl.semaphore_signal(barrier, inc=1, device_id={"vec": peer}, device_id_type=MESH)
    for side in range(2):
        @pl.when(has[side])
        def _(side=side):
            pl.semaphore_signal(barrier, inc=1, device_id={"lat": other[side]}, device_id_type=MESH)
        @pl.when(reaches[side])
        def _(side=side):
            pl.semaphore_signal(barrier, inc=1, device_id={"lat": far[side]}, device_id_type=MESH)
    pl.semaphore_wait(barrier, nv - 1 + sum(flag.astype(jnp.int32) for flag in has + reaches))

    def remote(src, dst, send, recv, target):
        return pltpu.make_async_remote_copy(
            src_ref=src, dst_ref=dst, send_sem=send, recv_sem=recv,
            device_id=target, device_id_type=MESH,
        )

    def edges(side):
        made = []
        for s in range(steps - 1):
            at = edge[side](reach - 1 - s)
            made.append(remote(
                wind.at[s, :, at, :], ring.at[v, s, pl.ds(0, 3), at, :],
                cs.at[side, s, 0], cr.at[side, s, 0], {"lat": other[side]}))
            made.append(remote(
                depth.at[s, at, :], ring.at[v, s, 3, at, :],
                cs.at[side, s, 1], cr.at[side, s, 1], {"lat": other[side]}))
        return made

    def state(side, k):
        at = edge[side](reach)
        return remote(
            x_hbm.at[k, :, at, :], halo.at[k, :, at, :],
            hs.at[side, k], hr.at[side, k], {"lat": other[side]})

    def detour(side, k):
        at = edge[side](reach)
        return remote(
            x_hbm.at[k, :, at, :], transit.at[k, :, at, :],
            hs.at[side, k], tr.at[k], {"lat": other[1 - side]})

    def onward(side, k):
        at = edge[side](reach)
        return remote(
            transit.at[k, :, at, :], halo.at[k, :, at, :],
            ts.at[k], hr.at[side, k], {"lat": far[side]})

    def spread(n, peer):
        return [
            remote(wind, own.at[v, :, pl.ds(0, 3)], gs.at[n, 0], gr.at[n, 0], {"vec": peer}),
            remote(depth, own.at[v, :, 3], gs.at[n, 1], gr.at[n, 1], {"vec": peer}),
        ]

    def passed(side, n, peer):
        made = []
        for s in range(steps - 1):
            at = edge[side](reach - 1 - s)
            made.append(remote(
                ring.at[v, s, :, at, :], ring.at[v, s, :, at, :],
                fs.at[side, n, s], fr.at[side, n, s], {"vec": peer}))
        return made

    for side in range(2):
        @pl.when(has[side])
        def _(side=side):
            for copy in edges(side):
                copy.start()

    @pl.loop(0, count)
    def _(k):
        for side in range(2):
            @pl.when(k < relayed[side])
            def _(side=side):
                detour(side, k).start()

    @pl.loop(0, count)
    def _(k):
        for side in range(2):
            @pl.when(has[side] & (k >= relayed[side]))
            def _(side=side):
                state(side, k).start()

    for n, peer in enumerate(peers):
        for copy in spread(n, peer):
            copy.start()

    for side in range(2):
        @pl.when(has[1 - side])
        def _(side=side):
            for copy in edges(side):
                copy.wait_recv()
            for n, peer in enumerate(peers):
                for copy in passed(side, n, peer):
                    copy.start()

    @pl.loop(0, count)
    def _(k):
        for side in range(2):
            @pl.when(k < relaying[side])
            def _(side=side):
                detour(side, k).wait_recv()
                onward(side, k).start()
    for copy in local:
        copy.wait()
    for n, peer in enumerate(peers):
        for copy in spread(n, peer):
            copy.wait_recv()
    for side in range(2):
        @pl.when(has[1 - side])
        def _(side=side):
            for n, peer in enumerate(peers):
                for copy in passed(side, n, peer):
                    copy.wait_recv()

    row = lax.broadcasted_iota(jnp.int32, (8, LANES), 0)

    @pl.loop(0, count)
    def _(k):
        for side in range(2):
            @pl.when(has[1 - side])
            def _(side=side):
                state(side, k).wait_recv()

        def span(t):
            return pl.ds(t * LANES, LANES)

        def first(side, f, t):
            return (x, halo)[side][k, f, :, span(t)]

        def reader(ref):
            return lambda side, f, t: ref[side, f, :, span(t)]

        def writer(ref):
            def put(side, f, t, value):
                ref[side, f, :, span(t)] = value
            return put

        def last(side, f, t, value):
            out[k, f, :, span(t)] = value

        for s in range(steps):
            def coefficient(side, channel, t, s=s):
                block, offset = divmod(t * LANES, part)
                return (own, ring)[side][block, s, channel, :, pl.ds(offset, LANES)]

            final = s == steps - 1
            good = reach - 1 - s
            keep = ((row < good) & has[1]) | ((row >= rows - good) & has[0])
            sweep(
                first if s == 0 else reader((ping, pong)[(s - 1) % 2]),
                last if final else writer((ping, pong)[s % 2]),
                coefficient, (0,) if final else (0, 1), tiles, keep)
        pltpu.make_async_copy(out.at[k], out_hbm.at[k], out_sem.at[k]).start()

    for side in range(2):
        @pl.when(has[side])
        def _(side=side):
            for copy in edges(side):
                copy.wait_send()
        @pl.when(has[1 - side])
        def _(side=side):
            for n, peer in enumerate(peers):
                for copy in passed(side, n, peer):
                    copy.wait_send()
    for n, peer in enumerate(peers):
        for copy in spread(n, peer):
            copy.wait_send()

    @pl.loop(0, count)
    def _(k):
        for side in range(2):
            @pl.when(has[side])
            def _(side=side):
                state(side, k).wait_send()
            @pl.when(k < relaying[side])
            def _(side=side):
                onward(side, k).wait_send()
        pltpu.make_async_copy(out.at[k], out_hbm.at[k], out_sem.at[k]).wait()


def solution(mesh):
    nv, nl = mesh.shape["vec"], mesh.shape["lat"]

    def shards(perturbation, wind_coriolis, depth_field):
        count, _, rows, width = perturbation.shape
        steps, part = wind_coriolis.shape[0], wind_coriolis.shape[3]
        dma = pltpu.SemaphoreType.DMA
        f32 = jnp.float32
        return pl.pallas_call(
            functools.partial(kernel, nv, nl),
            out_shape=jax.ShapeDtypeStruct(perturbation.shape, f32),
            in_specs=[pl.BlockSpec(memory_space=pltpu.HBM)] * 3,
            out_specs=pl.BlockSpec(memory_space=pl.ANY),
            scratch_shapes=[
                pltpu.VMEM((count, 3, rows, width), f32),
                pltpu.VMEM((count, 3, rows, width), f32),
                pltpu.VMEM((count, 3, rows, width), f32),
                pltpu.VMEM((2, 3, rows, width), f32),
                pltpu.VMEM((2, 3, rows, width), f32),
                pltpu.VMEM((count, 3, rows, width), f32),
                pltpu.VMEM((nv, steps, 4, rows, part), f32),
                pltpu.VMEM((nv, steps - 1, 4, rows, part), f32),
                dma((1,)), dma((2,)), dma((count,)),
                dma((nv - 1, 2)), dma((nv - 1, 2)),
                dma((2, steps - 1, 2)), dma((2, steps - 1, 2)),
                dma((2, nv - 1, steps - 1)), dma((2, nv - 1, steps - 1)),
                dma((2, count)), dma((2, count)), dma((count,)), dma((count,)),
            ],
            compiler_params=pltpu.CompilerParams(
                collective_id=0, has_side_effects=True, vmem_limit_bytes=40 * 1024 * 1024
            ),
        )(*(pltpu.with_memory_space_constraint(a, pltpu.HBM) for a in (perturbation, wind_coriolis, depth_field)))

    placed = (P("vec", None, "lat", None), P(None, None, "lat", "vec"), P(None, "lat", "vec"))
    return jax.shard_map(
        shards, mesh=mesh, in_specs=placed, out_specs=P("vec", None, "lat", None), check_vma=False
    )
```

```python
import functools

import jax
import jax.numpy as jnp
from jax import lax
from jax.experimental import pallas as pl
from jax.experimental.pallas import tpu as pltpu
from jax.sharding import PartitionSpec as P

MESH = pl.DeviceIdType.MESH
LANES = 128
time_step = 0.2
viscosity = 0.05
side_weight = time_step * viscosity
half_step = 0.5 * time_step


def sweep(load, store, coefficient, sides, tiles, keep):
    lane = lax.broadcasted_iota(jnp.int32, (8, LANES), 1)
    row = lax.broadcasted_iota(jnp.int32, (8, LANES), 0)
    first_lane, last_lane = lane == 0, lane == LANES - 1
    first_row, last_row = row == 0, row == 7
    known = {}

    def tile(side, field, t):
        key = (side, field, t)
        if key not in known:
            value = load(side, field, t % tiles)
            known[key] = (value, pltpu.roll(value, LANES - 1, 1), pltpu.roll(value, 1, 1))
        return known[key]

    for t in range(tiles):
        east, west, rise, fall, here = {}, {}, {}, {}, {}
        for field in range(3):
            turned = []
            for side in range(2):
                value = tile(side, field, t)[0] if side in sides else load(side, field, t)
                turned.append((pltpu.roll(value, 7, 0), pltpu.roll(value, 1, 0)))
            for side in sides:
                before, now, after = (tile(side, field, t + k) for k in (-1, 0, 1))
                here[side, field] = now[0]
                east[side, field] = jnp.where(last_lane, after[1], now[1])
                west[side, field] = jnp.where(first_lane, before[2], now[2])
                rise[side, field] = jnp.where(last_row, turned[1 - side][0], turned[side][0])
                fall[side, field] = jnp.where(first_row, turned[1 - side][1], turned[side][1])
        for side in sides:
            to_east, to_west, to_rise, to_fall, d, c = (coefficient(side, q, t) for q in range(6))
            new = [
                (1.0 - 4.0 * side_weight) * here[side, f]
                + (to_east * east[side, f] + to_west * west[side, f])
                + (to_rise * rise[side, f] + to_fall * fall[side, f])
                for f in range(3)
            ]
            new[0] -= c * ((east[side, 1] - west[side, 1]) + (rise[side, 2] - fall[side, 2]))
            new[1] += d * here[side, 2] - half_step * (east[side, 0] - west[side, 0])
            new[2] -= d * here[side, 1] + half_step * (rise[side, 0] - fall[side, 0])
            for f in range(3):
                store(side, f, t, new[f] if side == 0 else jnp.where(keep, new[f], 0.0))


def kernel(
    nv, nl, x_hbm, wind, depth, out,
    x, halo, transit, ping, pong, own, ring, table,
    x_sem, own_sem,
    gs, gr, cs, cr, fs, fr, hs, hr, ts, tr,
):
    count, _, rows, width = x_hbm.shape
    steps, part = wind.shape[0], wind.shape[3]
    tiles, reach = width // LANES, steps
    v, l = lax.axis_index("vec"), lax.axis_index("lat")
    has = (l > 0, l < nl - 1)
    other = (l - 1, l + 1)
    far = (l - 2, l + 2)
    reaches = (l > 1, l < nl - 2)
    pairs = nl // 2
    odd = lax.rem(l, 2)
    place = l // 2

    def share(number, wanted):
        return jnp.where(wanted, number * count // pairs, 0) if nl % 2 == 0 else jnp.int32(0)

    relayed = (
        share(place, (odd == 0) & reaches[0]),
        share(pairs - 1 - place, (odd == 1) & reaches[1]),
    )
    relaying = (
        share(place, (odd == 1) & reaches[0]),
        share(pairs - 1 - place, (odd == 0) & reaches[1]),
    )
    peers = [lax.rem(v + k, nv) for k in range(1, nv)]
    edge = (lambda n: pl.ds(0, n), lambda n: pl.ds(rows - n, n))

    local = [
        pltpu.make_async_copy(x_hbm, x, x_sem.at[0]),
        pltpu.make_async_copy(wind, own.at[v, :, pl.ds(0, 3)], own_sem.at[0]),
        pltpu.make_async_copy(depth, own.at[v, :, 3], own_sem.at[1]),
    ]
    for copy in local:
        copy.start()

    barrier = pltpu.get_barrier_semaphore()
    for peer in peers:
        pl.semaphore_signal(barrier, inc=1, device_id={"vec": peer}, device_id_type=MESH)
    for side in range(2):
        @pl.when(has[side])
        def _(side=side):
            pl.semaphore_signal(barrier, inc=1, device_id={"lat": other[side]}, device_id_type=MESH)
        @pl.when(reaches[side])
        def _(side=side):
            pl.semaphore_signal(barrier, inc=1, device_id={"lat": far[side]}, device_id_type=MESH)
    pl.semaphore_wait(barrier, nv - 1 + sum(flag.astype(jnp.int32) for flag in has + reaches))

    def remote(src, dst, send, recv, target):
        return pltpu.make_async_remote_copy(
            src_ref=src, dst_ref=dst, send_sem=send, recv_sem=recv,
            device_id=target, device_id_type=MESH,
        )

    def edges(side):
        made = []
        for s in range(steps - 1):
            at = edge[side](reach - 1 - s)
            made.append(remote(
                wind.at[s, :, at, :], ring.at[v, s, pl.ds(0, 3), at, :],
                cs.at[side, s, 0], cr.at[side, s, 0], {"lat": other[side]}))
            made.append(remote(
                depth.at[s, at, :], ring.at[v, s, 3, at, :],
                cs.at[side, s, 1], cr.at[side, s, 1], {"lat": other[side]}))
        return made

    def state(side, k):
        at = edge[side](reach)
        return remote(
            x_hbm.at[k, :, at, :], halo.at[k, :, at, :],
            hs.at[side, k], hr.at[side, k], {"lat": other[side]})

    def detour(side, k):
        at = edge[side](reach)
        return remote(
            x_hbm.at[k, :, at, :], transit.at[k, :, at, :],
            hs.at[side, k], tr.at[k], {"lat": other[1 - side]})

    def onward(side, k):
        at = edge[side](reach)
        return remote(
            transit.at[k, :, at, :], halo.at[k, :, at, :],
            ts.at[k], hr.at[side, k], {"lat": far[side]})

    def spread(n, peer):
        return [
            remote(wind, own.at[v, :, pl.ds(0, 3)], gs.at[n, 0], gr.at[n, 0], {"vec": peer}),
            remote(depth, own.at[v, :, 3], gs.at[n, 1], gr.at[n, 1], {"vec": peer}),
        ]

    def passed(side, n, peer):
        made = []
        for s in range(steps - 1):
            at = edge[side](reach - 1 - s)
            made.append(remote(
                ring.at[v, s, :, at, :], ring.at[v, s, :, at, :],
                fs.at[side, n, s], fr.at[side, n, s], {"vec": peer}))
        return made

    for side in range(2):
        @pl.when(has[side])
        def _(side=side):
            for copy in edges(side):
                copy.start()

    @pl.loop(0, count)
    def _(k):
        for side in range(2):
            @pl.when(k < relayed[side])
            def _(side=side):
                detour(side, k).start()

    @pl.loop(0, count)
    def _(k):
        for side in range(2):
            @pl.when(has[side] & (k >= relayed[side]))
            def _(side=side):
                state(side, k).start()

    for n, peer in enumerate(peers):
        for copy in spread(n, peer):
            copy.start()

    for side in range(2):
        @pl.when(jnp.logical_not(has[1 - side]))
        def _(side=side):
            halo[:, :, edge[side](reach), :] = jnp.zeros((count, 3, reach, width), jnp.float32)

    for side in range(2):
        @pl.when(has[1 - side])
        def _(side=side):
            for copy in edges(side):
                copy.wait_recv()
            for n, peer in enumerate(peers):
                for copy in passed(side, n, peer):
                    copy.start()

    @pl.loop(0, count)
    def _(k):
        for side in range(2):
            @pl.when(k < relaying[side])
            def _(side=side):
                detour(side, k).wait_recv()
                onward(side, k).start()
    for copy in local:
        copy.wait()
    for n, peer in enumerate(peers):
        for copy in spread(n, peer):
            copy.wait_recv()
    for side in range(2):
        @pl.when(has[1 - side])
        def _(side=side):
            for n, peer in enumerate(peers):
                for copy in passed(side, n, peer):
                    copy.wait_recv()

    for side in range(2):
        @pl.loop(0, steps - side)
        def _(s, side=side):
            for t in range(tiles):
                block, offset = divmod(t * LANES, part)
                given = (own, ring)[side]
                a, b, d, c = (given[block, s, q, :, pl.ds(offset, LANES)] for q in range(4))
                a, b = half_step * a, half_step * b
                values = (side_weight - a, side_weight + a, side_weight - b, side_weight + b, time_step * d, half_step * c)
                for q, value in enumerate(values):
                    table[side, s, q, :, pl.ds(t * LANES, LANES)] = value

    row = lax.broadcasted_iota(jnp.int32, (8, LANES), 0)

    @pl.loop(0, count)
    def _(k):
        for side in range(2):
            @pl.when(has[1 - side])
            def _(side=side):
                state(side, k).wait_recv()

        def span(t):
            return pl.ds(t * LANES, LANES)

        def first(side, f, t):
            return (x, halo)[side][k, f, :, span(t)]

        def reader(ref):
            return lambda side, f, t: ref[side, f, :, span(t)]

        def writer(ref):
            def put(side, f, t, value):
                ref[side, f, :, span(t)] = value
            return put

        def last(side, f, t, value):
            out[k, f, :, span(t)] = value

        for s in range(steps):
            def coefficient(side, channel, t, s=s):
                return table[side, s, channel, :, span(t)]

            final = s == steps - 1
            good = reach - 1 - s
            keep = ((row < good) & has[1]) | ((row >= rows - good) & has[0])
            sweep(
                first if s == 0 else reader((ping, pong)[(s - 1) % 2]),
                last if final else writer((ping, pong)[s % 2]),
                coefficient, (0,) if final else (0, 1), tiles, keep)

    for side in range(2):
        @pl.when(has[side])
        def _(side=side):
            for copy in edges(side):
                copy.wait_send()
        @pl.when(has[1 - side])
        def _(side=side):
            for n, peer in enumerate(peers):
                for copy in passed(side, n, peer):
                    copy.wait_send()
    for n, peer in enumerate(peers):
        for copy in spread(n, peer):
            copy.wait_send()

    @pl.loop(0, count)
    def _(k):
        for side in range(2):
            @pl.when(has[side])
            def _(side=side):
                state(side, k).wait_send()
            @pl.when(k < relaying[side])
            def _(side=side):
                onward(side, k).wait_send()


def solution(mesh):
    nv, nl = mesh.shape["vec"], mesh.shape["lat"]

    def shards(perturbation, wind_coriolis, depth_field):
        count, _, rows, width = perturbation.shape
        steps, part = wind_coriolis.shape[0], wind_coriolis.shape[3]
        dma = pltpu.SemaphoreType.DMA
        f32 = jnp.float32
        return pl.pallas_call(
            functools.partial(kernel, nv, nl),
            out_shape=jax.ShapeDtypeStruct(perturbation.shape, f32),
            in_specs=[pl.BlockSpec(memory_space=pltpu.HBM)] * 3,
            out_specs=pl.BlockSpec(memory_space=pltpu.VMEM),
            scratch_shapes=[
                pltpu.VMEM((count, 3, rows, width), f32),
                pltpu.VMEM((count, 3, rows, width), f32),
                pltpu.VMEM((count, 3, rows, width), f32),
                pltpu.VMEM((2, 3, rows, width), f32),
                pltpu.VMEM((2, 3, rows, width), f32),
                pltpu.VMEM((nv, steps, 4, rows, part), f32),
                pltpu.VMEM((nv, steps - 1, 4, rows, part), f32),
                pltpu.VMEM((2, steps, 6, rows, width), f32),
                dma((1,)), dma((2,)),
                dma((nv - 1, 2)), dma((nv - 1, 2)),
                dma((2, steps - 1, 2)), dma((2, steps - 1, 2)),
                dma((2, nv - 1, steps - 1)), dma((2, nv - 1, steps - 1)),
                dma((2, count)), dma((2, count)), dma((count,)), dma((count,)),
            ],
            compiler_params=pltpu.CompilerParams(
                collective_id=0, has_side_effects=True, vmem_limit_bytes=40 * 1024 * 1024
            ),
        )(*(pltpu.with_memory_space_constraint(a, pltpu.HBM) for a in (perturbation, wind_coriolis, depth_field)))

    placed = (P("vec", None, "lat", None), P(None, None, "lat", "vec"), P(None, "lat", "vec"))
    return jax.shard_map(
        shards, mesh=mesh, in_specs=placed, out_specs=P("vec", None, "lat", None), check_vma=False
    )
```

```python
import functools

import jax
import jax.numpy as jnp
from jax import lax
from jax.experimental import pallas as pl
from jax.experimental.pallas import tpu as pltpu
from jax.sharding import PartitionSpec as P

MESH = pl.DeviceIdType.MESH
LANES = 128
time_step = 0.2
viscosity = 0.05
side_weight = time_step * viscosity
half_step = 0.5 * time_step


def sweep(load, store, coefficient, sides, tiles, keep):
    lane = lax.broadcasted_iota(jnp.int32, (8, LANES), 1)
    row = lax.broadcasted_iota(jnp.int32, (8, LANES), 0)
    first_lane, last_lane = lane == 0, lane == LANES - 1
    first_row, last_row = row == 0, row == 7
    known = {}

    def tile(side, field, t):
        key = (side, field, t)
        if key not in known:
            value = load(side, field, t % tiles)
            known[key] = (value, pltpu.roll(value, LANES - 1, 1), pltpu.roll(value, 1, 1))
        return known[key]

    for t in range(tiles):
        east, west, rise, fall, here = {}, {}, {}, {}, {}
        for field in range(3):
            turned = []
            for side in range(2):
                value = tile(side, field, t)[0] if side in sides else load(side, field, t)
                turned.append((pltpu.roll(value, 7, 0), pltpu.roll(value, 1, 0)))
            for side in sides:
                before, now, after = (tile(side, field, t + k) for k in (-1, 0, 1))
                here[side, field] = now[0]
                east[side, field] = jnp.where(last_lane, after[1], now[1])
                west[side, field] = jnp.where(first_lane, before[2], now[2])
                rise[side, field] = jnp.where(last_row, turned[1 - side][0], turned[side][0])
                fall[side, field] = jnp.where(first_row, turned[1 - side][1], turned[side][1])
        for side in sides:
            to_east, to_west, to_rise, to_fall, d, c = (coefficient(side, q, t) for q in range(6))
            new = [
                (1.0 - 4.0 * side_weight) * here[side, f]
                + (to_east * east[side, f] + to_west * west[side, f])
                + (to_rise * rise[side, f] + to_fall * fall[side, f])
                for f in range(3)
            ]
            new[0] -= c * ((east[side, 1] - west[side, 1]) + (rise[side, 2] - fall[side, 2]))
            new[1] += d * here[side, 2] - half_step * (east[side, 0] - west[side, 0])
            new[2] -= d * here[side, 1] + half_step * (rise[side, 0] - fall[side, 0])
            for f in range(3):
                store(side, f, t, new[f] if side == 0 else jnp.where(keep, new[f], 0.0))


def kernel(
    nv, nl, x_hbm, wind, depth, out,
    x, halo, transit, ping, pong, own, ring, table,
    x_sem, own_sem,
    gs, gr, cs, cr, fs, fr, hs, hr, ts, tr,
):
    count, _, rows, width = x_hbm.shape
    steps, part = wind.shape[0], wind.shape[3]
    tiles, reach = width // LANES, steps
    v, l = lax.axis_index("vec"), lax.axis_index("lat")
    has = (l > 0, l < nl - 1)
    other = (l - 1, l + 1)
    far = (l - 2, l + 2)
    reaches = (l > 1, l < nl - 2)
    pairs = nl // 2
    odd = lax.rem(l, 2)
    place = l // 2

    def share(number, wanted):
        return jnp.where(wanted, number * count // pairs, 0) if nl % 2 == 0 else jnp.int32(0)

    relayed = (
        share(place, (odd == 0) & reaches[0]),
        share(pairs - 1 - place, (odd == 1) & reaches[1]),
    )
    relaying = (
        share(place, (odd == 1) & reaches[0]),
        share(pairs - 1 - place, (odd == 0) & reaches[1]),
    )
    peers = [lax.rem(v + k, nv) for k in range(1, nv)]
    edge = (lambda n: pl.ds(0, n), lambda n: pl.ds(rows - n, n))

    local = [
        pltpu.make_async_copy(x_hbm, x, x_sem.at[0]),
        pltpu.make_async_copy(wind, own.at[v, :, pl.ds(0, 3)], own_sem.at[0]),
        pltpu.make_async_copy(depth, own.at[v, :, 3], own_sem.at[1]),
    ]
    for copy in local:
        copy.start()

    barrier = pltpu.get_barrier_semaphore()
    for peer in peers:
        pl.semaphore_signal(barrier, inc=1, device_id={"vec": peer}, device_id_type=MESH)
    for side in range(2):
        @pl.when(has[side])
        def _(side=side):
            pl.semaphore_signal(barrier, inc=1, device_id={"lat": other[side]}, device_id_type=MESH)
        @pl.when(reaches[side])
        def _(side=side):
            pl.semaphore_signal(barrier, inc=1, device_id={"lat": far[side]}, device_id_type=MESH)
    pl.semaphore_wait(barrier, nv - 1 + sum(flag.astype(jnp.int32) for flag in has + reaches))

    def remote(src, dst, send, recv, target):
        return pltpu.make_async_remote_copy(
            src_ref=src, dst_ref=dst, send_sem=send, recv_sem=recv,
            device_id=target, device_id_type=MESH,
        )

    def edges(side):
        made = []
        for s in range(steps - 1):
            at = edge[side](reach - 1 - s)
            made.append(remote(
                wind.at[s, :, at, :], ring.at[v, s, pl.ds(0, 3), at, :],
                cs.at[side, s, 0], cr.at[side, s, 0], {"lat": other[side]}))
            made.append(remote(
                depth.at[s, at, :], ring.at[v, s, 3, at, :],
                cs.at[side, s, 1], cr.at[side, s, 1], {"lat": other[side]}))
        return made

    def state(side, k):
        at = edge[side](reach)
        return remote(
            x_hbm.at[k, :, at, :], halo.at[k, :, at, :],
            hs.at[side, k], hr.at[side, k], {"lat": other[side]})

    def detour(side, k):
        at = edge[side](reach)
        return remote(
            x_hbm.at[k, :, at, :], transit.at[k, :, at, :],
            hs.at[side, k], tr.at[k], {"lat": other[1 - side]})

    def onward(side, k):
        at = edge[side](reach)
        return remote(
            transit.at[k, :, at, :], halo.at[k, :, at, :],
            ts.at[k], hr.at[side, k], {"lat": far[side]})

    def spread(n, peer):
        return [
            remote(wind, own.at[v, :, pl.ds(0, 3)], gs.at[n, 0], gr.at[n, 0], {"vec": peer}),
            remote(depth, own.at[v, :, 3], gs.at[n, 1], gr.at[n, 1], {"vec": peer}),
        ]

    def passed(side, n, peer):
        made = []
        for s in range(steps - 1):
            at = edge[side](reach - 1 - s)
            made.append(remote(
                ring.at[v, s, :, at, :], ring.at[v, s, :, at, :],
                fs.at[side, n, s], fr.at[side, n, s], {"vec": peer}))
        return made

    for n, peer in enumerate(peers):
        for copy in spread(n, peer):
            copy.start()

    for side in range(2):
        @pl.when(has[side])
        def _(side=side):
            for copy in edges(side):
                copy.start()

    @pl.loop(0, count)
    def _(k):
        for side in range(2):
            @pl.when(k < relayed[side])
            def _(side=side):
                detour(side, k).start()
            @pl.when(has[side] & (odd == side) & (k >= relayed[side]))
            def _(side=side):
                state(side, k).start()

    @pl.loop(0, count)
    def _(k):
        for side in range(2):
            @pl.when(has[side] & (odd != side))
            def _(side=side):
                state(side, k).start()


    for side in range(2):
        @pl.when(jnp.logical_not(has[1 - side]))
        def _(side=side):
            halo[:, :, edge[side](reach), :] = jnp.zeros((count, 3, reach, width), jnp.float32)

    for side in range(2):
        @pl.when(has[1 - side])
        def _(side=side):
            for copy in edges(side):
                copy.wait_recv()
            for n, peer in enumerate(peers):
                for copy in passed(side, n, peer):
                    copy.start()

    @pl.loop(0, count)
    def _(k):
        for side in range(2):
            @pl.when(k < relaying[side])
            def _(side=side):
                detour(side, k).wait_recv()
                onward(side, k).start()
    for copy in local:
        copy.wait()
    for n, peer in enumerate(peers):
        for copy in spread(n, peer):
            copy.wait_recv()
    for side in range(2):
        @pl.when(has[1 - side])
        def _(side=side):
            for n, peer in enumerate(peers):
                for copy in passed(side, n, peer):
                    copy.wait_recv()

    for side in range(2):
        @pl.loop(0, steps - side)
        def _(s, side=side):
            for t in range(tiles):
                block, offset = divmod(t * LANES, part)
                given = (own, ring)[side]
                a, b, d, c = (given[block, s, q, :, pl.ds(offset, LANES)] for q in range(4))
                a, b = half_step * a, half_step * b
                values = (side_weight - a, side_weight + a, side_weight - b, side_weight + b, time_step * d, half_step * c)
                for q, value in enumerate(values):
                    table[side, s, q, :, pl.ds(t * LANES, LANES)] = value

    row = lax.broadcasted_iota(jnp.int32, (8, LANES), 0)

    @pl.loop(0, count)
    def _(k):
        for side in range(2):
            @pl.when(has[1 - side])
            def _(side=side):
                state(side, k).wait_recv()

        def span(t):
            return pl.ds(t * LANES, LANES)

        def first(side, f, t):
            return (x, halo)[side][k, f, :, span(t)]

        def reader(ref):
            return lambda side, f, t: ref[side, f, :, span(t)]

        def writer(ref):
            def put(side, f, t, value):
                ref[side, f, :, span(t)] = value
            return put

        def last(side, f, t, value):
            out[k, f, :, span(t)] = value

        for s in range(steps):
            def coefficient(side, channel, t, s=s):
                return table[side, s, channel, :, span(t)]

            final = s == steps - 1
            good = reach - 1 - s
            keep = ((row < good) & has[1]) | ((row >= rows - good) & has[0])
            sweep(
                first if s == 0 else reader((ping, pong)[(s - 1) % 2]),
                last if final else writer((ping, pong)[s % 2]),
                coefficient, (0,) if final else (0, 1), tiles, keep)

    for side in range(2):
        @pl.when(has[side])
        def _(side=side):
            for copy in edges(side):
                copy.wait_send()
        @pl.when(has[1 - side])
        def _(side=side):
            for n, peer in enumerate(peers):
                for copy in passed(side, n, peer):
                    copy.wait_send()
    for n, peer in enumerate(peers):
        for copy in spread(n, peer):
            copy.wait_send()

    @pl.loop(0, count)
    def _(k):
        for side in range(2):
            @pl.when(has[side])
            def _(side=side):
                state(side, k).wait_send()
            @pl.when(k < relaying[side])
            def _(side=side):
                onward(side, k).wait_send()


def solution(mesh):
    nv, nl = mesh.shape["vec"], mesh.shape["lat"]

    def shards(perturbation, wind_coriolis, depth_field):
        count, _, rows, width = perturbation.shape
        steps, part = wind_coriolis.shape[0], wind_coriolis.shape[3]
        dma = pltpu.SemaphoreType.DMA
        f32 = jnp.float32
        return pl.pallas_call(
            functools.partial(kernel, nv, nl),
            out_shape=jax.ShapeDtypeStruct(perturbation.shape, f32),
            in_specs=[pl.BlockSpec(memory_space=pltpu.HBM)] * 3,
            out_specs=pl.BlockSpec(memory_space=pltpu.VMEM),
            scratch_shapes=[
                pltpu.VMEM((count, 3, rows, width), f32),
                pltpu.VMEM((count, 3, rows, width), f32),
                pltpu.VMEM((count, 3, rows, width), f32),
                pltpu.VMEM((2, 3, rows, width), f32),
                pltpu.VMEM((2, 3, rows, width), f32),
                pltpu.VMEM((nv, steps, 4, rows, part), f32),
                pltpu.VMEM((nv, steps - 1, 4, rows, part), f32),
                pltpu.VMEM((2, steps, 6, rows, width), f32),
                dma((1,)), dma((2,)),
                dma((nv - 1, 2)), dma((nv - 1, 2)),
                dma((2, steps - 1, 2)), dma((2, steps - 1, 2)),
                dma((2, nv - 1, steps - 1)), dma((2, nv - 1, steps - 1)),
                dma((2, count)), dma((2, count)), dma((count,)), dma((count,)),
            ],
            compiler_params=pltpu.CompilerParams(
                collective_id=0, has_side_effects=True, vmem_limit_bytes=40 * 1024 * 1024
            ),
        )(*(pltpu.with_memory_space_constraint(a, pltpu.HBM) for a in (perturbation, wind_coriolis, depth_field)))

    placed = (P("vec", None, "lat", None), P(None, None, "lat", "vec"), P(None, "lat", "vec"))
    return jax.shard_map(
        shards, mesh=mesh, in_specs=placed, out_specs=P("vec", None, "lat", None), check_vma=False
    )
```
